32 devices in a mesh: groups: 2 (over x), tm: 16 (over z, y, core).
Axes of the slice: x: 2, y: 2, z: 4, core: 2. Of those that a mesh axis runs over, the one named last changes fastest.
Arguments:
- queries: bfloat16 [6144, 2560], P(('groups', 'tm')), parts along dimension 0, may hold values from -6 to 6
- keys: bfloat16 [6144, 2560], P(('groups', 'tm')), parts along dimension 0, may hold values from -6 to 6
- values: bfloat16 [6144, 2560], P(('groups', 'tm')), parts along dimension 0, may hold values from -6 to 6
- q_gain: float32 [2560], replicated, may hold values from 0.5 to 1.5
- k_gain: float32 [2560], replicated, may hold values from 0.5 to 1.5
- out_weight: bfloat16 [2560, 5120], P('tm'), may hold values from -0.125 to 0.125
- out_gate: float32 [5120], replicated, may hold values from 0.5 to 2
- reach: int32 [32, 2], P(('groups', 'tm')), parts along dimension 0, may hold values from 0 to 1
Outputs:
- mixed: bfloat16 [6144, 5120], P(('groups', 'tm')), parts along dimension 0
The draws below stay inside these ranges and needn't reach their ends.
There are 2 independent parts, one for each index of `groups`. The reference program is written for one: setup_inputs(seed, part) draws one part's arguments, and reference() takes and returns one part's arrays. A program takes and returns all parts, laid end to end along the dimension named above; an argument that names none is the same for every part. Nothing has to cross between parts.
Inputs may be any that keep to these rules, and one draw needn't show every extreme that they name: `reach`: requests past the first or last tile are ignored.
All inputs are finite; a program needn't handle non-finite values.
Results may differ from the reference program's by a relative error of at most 0.0076.
Values may be sent and summed in bfloat16 or wider, within the bound.
A program may use at most 128 MiB of HBM per device.

```python
import math
import jax
import jax.numpy as jnp
from jax import lax

D = 5120
HEADS = 20
HD = 128
TT = 4
TH = 6
TW = 8
TILES = 16
TOKENS = 3072
CHANNELS = 2560


def draw_queries(key, part):
    base = jnp.clip(jax.random.normal(jax.random.fold_in(key, 711), (TOKENS, HEADS * HD), jnp.float32), -6.0, 6.0)
    return base.astype(jnp.bfloat16)


def draw_keys(key, part):
    base = jnp.clip(jax.random.normal(jax.random.fold_in(key, 712), (TOKENS, HEADS * HD), jnp.float32), -6.0, 6.0)
    return base.astype(jnp.bfloat16)


def place_ends(drawn, own_key, least, top_value):
    longest = drawn.shape.index(max(drawn.shape))
    spots = []
    for shift in (0, 1):
        where = [jax.random.randint(jax.random.fold_in(own_key, axis), (), 0, length) for axis, length in enumerate(drawn.shape)]
        where[longest] = (where[longest] + shift) % drawn.shape[longest]
        spots.append(tuple(where))
    return drawn.at[spots[0]].set(least).at[spots[1]].set(top_value)


def block_levels(key, shape, cuts, low, largest):
    level, own = 1.0, jax.random.fold_in(key, 6)
    for axis_at, shards_of in cuts:
        draws = jnp.exp(jax.random.uniform(jax.random.fold_in(own, axis_at), (shards_of,), jnp.float32, low / len(cuts), largest / len(cuts)))
        level = level * jnp.repeat(draws, shape[axis_at] // shards_of).reshape([-1 if axis == axis_at else 1 for axis in range(len(shape))])
    return level


def normal_values(key, shape, scale, most, shards=(), kind=jnp.bfloat16):
    values = jax.random.normal(key, shape, jnp.float32) * scale
    if len(shards) > 0:
        values = block_levels(key, shape, shards, -0.22, 0.18) * values
    return jnp.clip(values, min=-most, max=most).astype(kind)


def setup_inputs(seed: int = 0, part: int = 0) -> dict:
    arg_keys = jax.random.split(jax.random.key(seed), 9)
    own_keys = jax.random.split(jax.random.fold_in(arg_keys[8], part), 9)
    queries = draw_queries(jax.random.fold_in(jax.random.fold_in(arg_keys[8], part), 71), part)
    keys = draw_keys(jax.random.fold_in(jax.random.fold_in(arg_keys[8], part), 71), part)
    values = normal_values(own_keys[2], (TOKENS, CHANNELS), 1.0, 6.0, ((0, 16),))
    q_gain = jnp.clip(1.0 + 0.1 * jax.random.normal(arg_keys[3], (CHANNELS,), jnp.float32), 0.5, 1.5)
    k_gain = jnp.clip(1.0 + 0.1 * jax.random.normal(arg_keys[4], (CHANNELS,), jnp.float32), 0.5, 1.5)
    out_weight = normal_values(arg_keys[5], (CHANNELS, D), CHANNELS ** -0.5, 0.125, ((0, 16),))
    out_gate = jnp.clip(jnp.exp(jax.random.uniform(arg_keys[6], (D,), jnp.float32, math.log(0.5), math.log(2.0))), 0.5, 2.0)
    reach = place_ends(jax.random.randint(own_keys[7], (TILES, 2), 0, 2), jax.random.fold_in(own_keys[7], 1), 0, 1).astype(jnp.int32)
    return dict(queries=queries, keys=keys, values=values, q_gain=q_gain, k_gain=k_gain, out_weight=out_weight, out_gate=out_gate, reach=reach)


def rms_scaled(block, gain):
    values32 = block.astype(jnp.float32)
    inverse = lax.rsqrt(lax.optimization_barrier(jnp.mean(values32 * values32, axis=-1, keepdims=True)) + 1e-06)
    return (values32 * inverse * gain).astype(jnp.bfloat16)

def reference(queries, keys, values, q_gain, k_gain, out_weight, out_gate, reach):
    tile = TT * TH * TW
    scale = HD ** (-0.5)
    q_norm = rms_scaled(queries, q_gain).reshape(TILES, tile, HEADS, HD)
    k_norm = rms_scaled(keys, k_gain).reshape(TILES, tile, HEADS, HD)
    v_tiles = values.reshape(TILES, tile, HEADS, HD)
    padding = jnp.zeros((1, tile, HEADS, HD), jnp.bfloat16)
    key_tiles = jnp.concatenate([padding, k_norm, padding], axis=0)
    val_tiles = jnp.concatenate([padding, v_tiles, padding], axis=0)
    tile_index = jnp.arange(TILES, dtype=jnp.int32)
    valid = jnp.stack([(reach[:, 0] == 1) & (tile_index > 0), tile_index >= 0, (reach[:, 1] == 1) & (tile_index < TILES - 1)], axis=1)

    def one_tile(index):
        index = index.astype(jnp.int32)
        query = q_norm[index].astype(jnp.float32)
        seen_k = lax.dynamic_slice_in_dim(key_tiles, index, 3, 0).reshape(3 * tile, HEADS, HD).astype(jnp.float32)
        seen_v = lax.dynamic_slice_in_dim(val_tiles, index, 3, 0).reshape(3 * tile, HEADS, HD).astype(jnp.float32)
        logits = jnp.einsum('qhd,khd->hqk', query, seen_k) * scale
        mask = jnp.repeat(valid[index], tile)
        logits = jnp.where(mask[None, None, :], logits, -1e+30)
        top = lax.optimization_barrier(jnp.max(logits, axis=-1, keepdims=True))
        expo = jnp.exp(logits - top)
        weights = (expo / lax.optimization_barrier(jnp.sum(expo, axis=-1, keepdims=True))).astype(jnp.bfloat16)
        attended = jnp.einsum('hqk,khd->qhd', weights.astype(jnp.float32), seen_v).astype(jnp.bfloat16)
        attended = attended.reshape(tile, HEADS * HD)
        projected = jnp.dot(attended, out_weight, preferred_element_type=jnp.float32)
        return (out_gate * projected).astype(jnp.bfloat16)
    mixed = lax.map(one_tile, tile_index)
    return mixed.reshape(TOKENS, D)
```

```python
import functools

import jax
import jax.numpy as jnp
from jax import lax
from jax.experimental import pallas as pl
from jax.experimental.pallas import tpu as pltpu
from jax.sharding import PartitionSpec as P

HD = 128
TT = 4
TH = 6
TW = 8
MESH = pl.DeviceIdType.MESH


def shifted(shard, axis, by):
    peers = lax.axis_size(axis)
    pairs = [(i, i + by) for i in range(peers) if 0 <= i + by < peers]
    return lax.ppermute(shard, axis, pairs)


def rms_scaled(block, gain):
    values32 = block.astype(jnp.float32)
    inverse = lax.rsqrt(jnp.mean(values32 * values32, axis=-1, keepdims=True) + 1e-06)
    return (values32 * inverse * gain).astype(jnp.bfloat16)


def local(queries, keys, values, q_gain, k_gain, out_weight, out_gate, reach):
    tile = TT * TH * TW
    rows = queries.shape[0]
    chans = queries.shape[1]
    heads = chans // HD
    count = rows // tile
    scale = HD ** (-0.5)
    q_norm = rms_scaled(queries, q_gain)
    k_norm = rms_scaled(keys, k_gain)
    before_k, before_v = shifted((k_norm, values), "tm", 1)
    after_k, after_v = shifted((k_norm, values), "tm", -1)
    key_buffer = jnp.concatenate([before_k, k_norm, after_k], axis=0).reshape(
        count + 2, tile, heads, HD
    )
    val_buffer = jnp.concatenate([before_v, values, after_v], axis=0).reshape(
        count + 2, tile, heads, HD
    )
    position = lax.axis_index("tm")
    first_tile = position * count
    total_tiles = lax.axis_size("tm") * count
    global_tile = first_tile + jnp.arange(count, dtype=jnp.int32)
    valid = jnp.stack(
        [
            (reach[:, 0] == 1) & (global_tile > 0),
            global_tile >= 0,
            (reach[:, 1] == 1) & (global_tile < total_tiles - 1),
        ],
        axis=1,
    )
    query_tiles = q_norm.reshape(count, tile, heads, HD)
    seen_k = jnp.stack([key_buffer[offset : offset + count] for offset in range(3)], axis=1)
    seen_v = jnp.stack([val_buffer[offset : offset + count] for offset in range(3)], axis=1)
    logits = (
        jnp.einsum("nqhd,nokhd->nhqok", query_tiles, seen_k, preferred_element_type=jnp.float32)
        * scale
    )
    logits = jnp.where(valid[:, None, None, :, None], logits, -1e30)
    logits = logits.reshape(count, heads, tile, 3 * tile)
    top = jnp.max(logits, axis=-1, keepdims=True)
    expo = jnp.exp(logits - top)
    weights = (expo / jnp.sum(expo, axis=-1, keepdims=True)).astype(jnp.bfloat16)
    attended = jnp.einsum(
        "nhqk,nkhd->nqhd",
        weights,
        seen_v.reshape(count, 3 * tile, heads, HD),
        preferred_element_type=jnp.float32,
    ).astype(jnp.bfloat16)
    attended = attended.reshape(rows, chans)
    full_weight = lax.all_gather(out_weight, "tm", axis=0, tiled=True)
    projected = jnp.dot(attended, full_weight, preferred_element_type=jnp.float32)
    return (out_gate * projected).astype(jnp.bfloat16)


def lane_pieces(half):
    lanes = half // 256
    last = max(lanes // 5, 1)
    first = (lanes - last + 1) // 2
    widths = [w * 128 for w in (first, lanes - last - first, last) if w > 0]
    offsets, at = [], 0
    for w in widths:
        offsets.append(at)
        at += 2 * w
    return list(zip(offsets, widths))


def fused_kernel(
    ring, q_ref, k_ref, v_ref, qg_ref, kg_ref, w_ref, gate_ref, reach_ref, o_ref,
    wbuf, kbuf, vbuf, qn, att, sbuf,
    ring_ss, ring_rs, chip_ss, chip_rs, own_ss, own_rs, halo_ss, halo_rs,
    att_ss, att_rs, out_ss, out_rs, local_sem,
):
    rows, chans = q_ref.shape
    depth, wide = w_ref.shape
    half = wide // 2
    heads = chans // HD
    pieces = lane_pieces(half)
    far = ring // 2
    tiles = 2 * ring
    g, t = lax.axis_index("groups"), lax.axis_index("tm")
    core, chip = t % 2, t // 2
    row, col = chip // 2, chip % 2
    pos = row * (1 - col) + (ring - 1 - row) * col
    col0 = (g % 2) * half

    def chip_at(place):
        back = place // far
        line = place * (1 - back) + (ring - 1 - place) * back
        return 2 * line + back

    def peer(group, tm):
        return (group, tm)

    nxt = peer(g, 2 * chip_at((pos + 1) % ring) + core)
    prv = peer(g, 2 * chip_at((pos + ring - 1) % ring) + core)
    mate = peer(g, 2 * chip + 1 - core)
    cross = peer(g + 1 - 2 * (g % 2), t)
    outside = t - 1 + 2 * core
    has_outside = (outside >= 0) & (outside < tiles)

    def remote(src, dst, ss, rs, dev):
        return pltpu.make_async_remote_copy(
            src_ref=src, dst_ref=dst, send_sem=ss, recv_sem=rs, device_id=dev, device_id_type=MESH
        )

    barrier = pltpu.get_barrier_semaphore()
    for dev in (nxt, prv, mate, cross):
        pl.semaphore_signal(barrier, inc=1, device_id=dev, device_id_type=MESH)

    @pl.when(has_outside)
    def _():
        pl.semaphore_signal(barrier, inc=1, device_id=peer(g, outside), device_id_type=MESH)
        pl.semaphore_wait(barrier, 5)

    @pl.when(jnp.logical_not(has_outside))
    def _():
        pl.semaphore_wait(barrier, 4)

    def halo(side):
        to = peer(g, t + (1 if side else -1))
        there = pl.ds((0 if side else 2) * rows, rows)
        return [
            remote(k_ref, kbuf.at[there], halo_ss.at[side, 0], halo_rs.at[side, 0], to),
            remote(v_ref, vbuf.at[there], halo_ss.at[side, 1], halo_rs.at[side, 1], to),
        ]

    not_first, not_last = t > 0, t < tiles - 1

    @pl.when(not_last)
    def _():
        for c in halo(1):
            c.start()

    @pl.when(not_first)
    def _():
        for c in halo(0):
            c.start()

    own_rows = pl.ds(pl.multiple_of(t * depth, 16), depth)
    own_cols = pl.ds(pl.multiple_of(col0, 128), half)
    local_w = pltpu.make_async_copy(w_ref.at[:, own_cols], wbuf.at[own_rows], local_sem.at[0])
    local_v = pltpu.make_async_copy(v_ref, vbuf.at[pl.ds(rows, rows)], local_sem.at[1])
    local_w.start()
    local_v.start()
    own_out = remote(w_ref.at[:, own_cols], wbuf.at[own_rows], own_ss, own_rs, mate)
    own_out.start()

    def shard_rows(d, s, c):
        place = (pos + (ring - s if d == 0 else s)) % ring
        return pl.ds(pl.multiple_of((2 * chip_at(place) + c) * depth, 16), depth)

    def used(d, s, q):
        return s < far or (s == far and q == d)

    def lanes(f, q):
        off, w = pieces[f]
        return pl.ds(off + q * w, w)

    def ring_send(d, f, s, q):
        off, w = pieces[f]
        if s == 1:
            src = w_ref.at[:, pl.ds(pl.multiple_of(col0 + off + q * w, 128), w)]
            where = own_rows
        else:
            where = shard_rows(d, s - 1, core)
            src = wbuf.at[where, lanes(f, q)]
        return remote(
            src, wbuf.at[where, lanes(f, q)], ring_ss.at[d, f, s - 1, q], ring_rs.at[d, f, s - 1, q],
            nxt if d == 0 else prv,
        )

    def ring_recv(d, f, s, q):
        here = wbuf.at[shard_rows(d, s, core), lanes(f, q)]
        return remote(here, here, ring_ss.at[d, f, s - 1, q], ring_rs.at[d, f, s - 1, q], nxt)

    def chip_copy(d, f, s, q, c):
        here = wbuf.at[shard_rows(d, s, c), lanes(f, q)]
        return remote(here, here, chip_ss.at[d, f, s - 1, q], chip_rs.at[d, f, s - 1, q], mate)

    def launch(f):
        for q in (0, 1):
            for d in (0, 1):
                if used(d, 1, q):
                    ring_send(d, f, 1, q).start()

    def ring_step(f, s):
        for q in (0, 1):
            for d in (0, 1):
                if used(d, s, q):
                    ring_recv(d, f, s, q).wait_recv()
                    if s < far and used(d, s + 1, q):
                        ring_send(d, f, s + 1, q).start()
                    chip_copy(d, f, s, q, core).start()
        if s == max(far - 1, 1) and f + 1 < len(pieces):
            launch(f + 1)

    launch(0)

    def normed(x, gain):
        x = x.astype(jnp.float32)
        inverse = lax.rsqrt(jnp.mean(x * x, axis=-1, keepdims=True) + 1e-06)
        return (x * inverse * gain).astype(jnp.bfloat16)

    step_rows = 32

    def normalise(src, src0, dst, dst0, gain):
        @pl.loop(0, rows // step_rows)
        def _(i):
            x = src[pl.ds(pl.multiple_of(src0 + i * step_rows, 16), step_rows), :]
            dst[pl.ds(pl.multiple_of(dst0 + i * step_rows, 16), step_rows), :] = normed(x, gain[...])

    normalise(q_ref, 0, qn, 0, qg_ref)
    normalise(k_ref, 0, kbuf, rows, kg_ref)

    see_before = (reach_ref[0, 0] == 1) & not_first
    see_after = (reach_ref[0, 1] == 1) & not_last
    column = lax.broadcasted_iota(jnp.int32, (1, 3 * rows), 1)
    lowest = jnp.where(see_before, 0, rows)
    highest = jnp.where(see_after, 3 * rows, 2 * rows)
    seen = (column >= lowest) & (column < highest)

    def head(h):
        at = pl.ds(pl.multiple_of(h * HD, 128), HD)
        logits = lax.dot_general(
            qn[:, at], kbuf[:, at], (((1,), (1,)), ((), ())), preferred_element_type=jnp.float32
        ) * (HD ** (-0.5))
        logits = jnp.where(seen, logits, -1e30)
        top = jnp.max(logits, axis=-1, keepdims=True)
        expo = jnp.exp(logits - top)
        weights = (expo * (1.0 / jnp.sum(expo, axis=-1, keepdims=True))).astype(jnp.bfloat16)
        att[0:rows, at] = jnp.dot(
            weights, vbuf[:, at], preferred_element_type=jnp.float32
        ).astype(jnp.bfloat16)

    groups_of = 4 if heads % 4 == 0 else 1
    per = heads // groups_of

    def attention(i):
        @pl.loop(0, per)
        def _(j):
            head(i * per + j)

    def att_send(i):
        at = pl.ds(i * per * HD, per * HD)
        return remote(
            att.at[pl.ds(0, rows), at], att.at[pl.ds(rows, rows), at], att_ss.at[i], att_rs.at[i], cross
        )

    def wait_halo():
        local_v.wait()

        @pl.when(not_first)
        def _():
            for c in halo(1):
                c.wait_recv()
            normalise(kbuf, 0, kbuf, 0, kg_ref)

        @pl.when(t == 0)
        def _():
            kbuf[0:rows] = jnp.zeros((rows, chans), jnp.bfloat16)
            vbuf[0:rows] = jnp.zeros((rows, chans), jnp.bfloat16)

        @pl.when(not_last)
        def _():
            for c in halo(0):
                c.wait_recv()
            normalise(kbuf, 2 * rows, kbuf, 2 * rows, kg_ref)

        @pl.when(t == tiles - 1)
        def _():
            kbuf[2 * rows : 3 * rows] = jnp.zeros((rows, chans), jnp.bfloat16)
            vbuf[2 * rows : 3 * rows] = jnp.zeros((rows, chans), jnp.bfloat16)

    def out_send(f):
        off, w = pieces[f]
        there = pl.ds(pl.multiple_of(col0 + off, 128), 2 * w)
        return remote(
            sbuf.at[:, pl.ds(off, 2 * w)], o_ref.at[:, there], out_ss.at[f], out_rs.at[f], cross
        )

    def out_recv(f):
        off, w = pieces[f]
        there = pl.ds(pl.multiple_of(half - col0 + off, 128), 2 * w)
        return remote(o_ref.at[:, there], o_ref.at[:, there], out_ss.at[f], out_rs.at[f], cross)

    def project(f):
        off, w = pieces[f]
        for s in range(1, far + 1):
            for q in (0, 1):
                for d in (0, 1):
                    if used(d, s, q):
                        chip_copy(d, f, s, q, 1 - core).wait_recv()
        block = 256

        @pl.loop(0, 2 * w // block)
        def _(j):
            at = pl.ds(pl.multiple_of(off + j * block, 128), block)
            out_at = pl.ds(pl.multiple_of(col0 + off + j * block, 128), block)
            total = jnp.dot(att[...], wbuf[:, at], preferred_element_type=jnp.float32)
            scaled = (gate_ref[:, out_at] * total).astype(jnp.bfloat16)
            sbuf[:, at] = scaled[rows:]
            o_ref[:, out_at] = scaled[:rows]

        out_send(f).start()

    queue = [(f, s) for f in range(len(pieces)) for s in range(1, far + 1)]
    ring_step(*queue.pop(0))
    wait_halo()
    for i in range(groups_of):
        attention(i)
        if i > 0:
            att_send(i - 1).start()
        if queue:
            ring_step(*queue.pop(0))
    att_send(groups_of - 1).start()
    local_w.wait()
    first_wait = True
    todo = list(range(len(pieces)))
    while todo:
        f = todo[0]
        while queue and (queue[0][0] <= f or (queue[0][0] == f + 1 and queue[0][1] <= min(2, far))):
            ring_step(*queue.pop(0))
        if first_wait:
            remote(
                w_ref.at[:, own_cols],
                wbuf.at[pl.ds(pl.multiple_of((2 * chip + 1 - core) * depth, 16), depth)],
                own_ss, own_rs, mate,
            ).wait_recv()
            for i in range(groups_of):
                att_send(i).wait_recv()
            first_wait = False
        project(f)
        todo.pop(0)

    own_out.wait_send()

    @pl.when(not_last)
    def _():
        for c in halo(1):
            c.wait_send()

    @pl.when(not_first)
    def _():
        for c in halo(0):
            c.wait_send()

    for i in range(groups_of):
        att_send(i).wait_send()
    for f in range(len(pieces)):
        for s in range(1, far + 1):
            for q in (0, 1):
                for d in (0, 1):
                    if used(d, s, q):
                        ring_send(d, f, s, q).wait_send()
                        chip_copy(d, f, s, q, core).wait_send()
    for f in range(len(pieces)):
        out_send(f).wait_send()
        out_recv(f).wait_recv()


def fused(peers, queries, keys, values, q_gain, k_gain, out_weight, out_gate, reach):
    rows, chans = queries.shape
    depth, wide = out_weight.shape
    half = wide // 2
    ring = peers // 2
    far = ring // 2
    parts = len(lane_pieces(half))
    groups_of = 4 if (chans // HD) % 4 == 0 else 1
    dma = pltpu.SemaphoreType.DMA
    vmem = pl.BlockSpec(memory_space=pltpu.VMEM)
    return pl.pallas_call(
        functools.partial(fused_kernel, ring),
        out_shape=jax.ShapeDtypeStruct((rows, wide), jnp.bfloat16),
        in_specs=[vmem] * 7 + [pl.BlockSpec(memory_space=pltpu.SMEM)],
        out_specs=vmem,
        scratch_shapes=[
            pltpu.VMEM((depth * peers, half), jnp.bfloat16),
            pltpu.VMEM((3 * rows, chans), jnp.bfloat16),
            pltpu.VMEM((3 * rows, chans), jnp.bfloat16),
            pltpu.VMEM((rows, chans), jnp.bfloat16),
            pltpu.VMEM((2 * rows, chans), jnp.bfloat16),
            pltpu.VMEM((rows, half), jnp.bfloat16),
            dma((2, parts, far, 2)),
            dma((2, parts, far, 2)),
            dma((2, parts, far, 2)),
            dma((2, parts, far, 2)),
            dma, dma,
            dma((2, 2)), dma((2, 2)),
            dma((groups_of,)), dma((groups_of,)),
            dma((parts,)), dma((parts,)),
            dma((2,)),
        ],
        compiler_params=pltpu.CompilerParams(
            collective_id=0, has_side_effects=True, vmem_limit_bytes=60 * 1024 * 1024
        ),
    )(
        queries, keys, values, q_gain.reshape(1, -1), k_gain.reshape(1, -1), out_weight,
        out_gate.reshape(1, -1), reach,
    )


def solution(mesh):
    groups, peers = mesh.shape["groups"], mesh.shape["tm"]

    def step(queries, keys, values, q_gain, k_gain, out_weight, out_gate, reach):
        fits = (
            groups % 2 == 0
            and peers % 8 == 0
            and queries.shape[0] == TT * TH * TW
            and out_weight.shape[0] % 16 == 0
            and out_weight.shape[1] % 512 == 0
        )
        args = (queries, keys, values, q_gain, k_gain, out_weight, out_gate, reach)
        return fused(peers, *args) if fits else local(*args)

    return jax.shard_map(
        step,
        mesh=mesh,
        in_specs=(
            P(("groups", "tm"), None),
            P(("groups", "tm"), None),
            P(("groups", "tm"), None),
            P(),
            P(),
            P("tm", None),
            P(),
            P(("groups", "tm"), None),
        ),
        out_specs=P(("groups", "tm"), None),
        check_vma=False,
    )
```

```python
import functools

import jax
import jax.numpy as jnp
from jax import lax
from jax.experimental import pallas as pl
from jax.experimental.pallas import tpu as pltpu
from jax.sharding import PartitionSpec as P

HD = 128
TT = 4
TH = 6
TW = 8
MESH = pl.DeviceIdType.MESH
SCHEDULE = ("H0", "L", "H1", "H2", "H3", "R", "Y0", "R", "Y1", "A", "R", "Y2", "A", "R", "Y3", "A", "R", "A", "R", "S", "R", "P", "R", "R", "P", "R", "R", "P")


def shifted(shard, axis, by):
    peers = lax.axis_size(axis)
    pairs = [(i, i + by) for i in range(peers) if 0 <= i + by < peers]
    return lax.ppermute(shard, axis, pairs)


def rms_scaled(block, gain):
    values32 = block.astype(jnp.float32)
    inverse = lax.rsqrt(jnp.mean(values32 * values32, axis=-1, keepdims=True) + 1e-06)
    return (values32 * inverse * gain).astype(jnp.bfloat16)


def local(queries, keys, values, q_gain, k_gain, out_weight, out_gate, reach):
    tile = TT * TH * TW
    rows = queries.shape[0]
    chans = queries.shape[1]
    heads = chans // HD
    count = rows // tile
    scale = HD ** (-0.5)
    q_norm = rms_scaled(queries, q_gain)
    k_norm = rms_scaled(keys, k_gain)
    before_k, before_v = shifted((k_norm, values), "tm", 1)
    after_k, after_v = shifted((k_norm, values), "tm", -1)
    key_buffer = jnp.concatenate([before_k, k_norm, after_k], axis=0).reshape(
        count + 2, tile, heads, HD
    )
    val_buffer = jnp.concatenate([before_v, values, after_v], axis=0).reshape(
        count + 2, tile, heads, HD
    )
    position = lax.axis_index("tm")
    first_tile = position * count
    total_tiles = lax.axis_size("tm") * count
    global_tile = first_tile + jnp.arange(count, dtype=jnp.int32)
    valid = jnp.stack(
        [
            (reach[:, 0] == 1) & (global_tile > 0),
            global_tile >= 0,
            (reach[:, 1] == 1) & (global_tile < total_tiles - 1),
        ],
        axis=1,
    )
    query_tiles = q_norm.reshape(count, tile, heads, HD)
    seen_k = jnp.stack([key_buffer[offset : offset + count] for offset in range(3)], axis=1)
    seen_v = jnp.stack([val_buffer[offset : offset + count] for offset in range(3)], axis=1)
    logits = (
        jnp.einsum("nqhd,nokhd->nhqok", query_tiles, seen_k, preferred_element_type=jnp.float32)
        * scale
    )
    logits = jnp.where(valid[:, None, None, :, None], logits, -1e30)
    logits = logits.reshape(count, heads, tile, 3 * tile)
    top = jnp.max(logits, axis=-1, keepdims=True)
    expo = jnp.exp(logits - top)
    weights = (expo / jnp.sum(expo, axis=-1, keepdims=True)).astype(jnp.bfloat16)
    attended = jnp.einsum(
        "nhqk,nkhd->nqhd",
        weights,
        seen_v.reshape(count, 3 * tile, heads, HD),
        preferred_element_type=jnp.float32,
    ).astype(jnp.bfloat16)
    attended = attended.reshape(rows, chans)
    full_weight = lax.all_gather(out_weight, "tm", axis=0, tiled=True)
    projected = jnp.dot(attended, full_weight, preferred_element_type=jnp.float32)
    return (out_gate * projected).astype(jnp.bfloat16)


def lane_pieces(half):
    lanes = half // 256
    last = max(lanes // 5, 1)
    first = (lanes - last + 1) // 2
    widths = [w * 128 for w in (first, lanes - last - first, last) if w > 0]
    offsets, at = [], 0
    for w in widths:
        offsets.append(at)
        at += 2 * w
    return list(zip(offsets, widths))


def fused_kernel(
    ring, q_ref, k_ref, v_ref, qg_ref, kg_ref, w_ref, gate_ref, reach_ref, o_ref,
    wbuf, kbuf, vbuf, held, qn, att, sbuf,
    ring_ss, ring_rs, chip_ss, chip_rs, own_ss, own_rs, mate_ss, mate_rs, side_ss, side_rs, relay_ss, relay_rs,
    att_ss, att_rs, out_ss, out_rs, local_sem,
):
    rows, chans = q_ref.shape
    depth, wide = w_ref.shape
    half = wide // 2
    heads = chans // HD
    pieces = lane_pieces(half)
    far = ring // 2
    tiles = 2 * ring
    g, t = lax.axis_index("groups"), lax.axis_index("tm")
    core, chip = t % 2, t // 2
    row, col = chip // 2, chip % 2
    pos = row * (1 - col) + (ring - 1 - row) * col
    col0 = (g % 2) * half

    def chip_at(place):
        back = place // far
        line = place * (1 - back) + (ring - 1 - place) * back
        return 2 * line + back

    def peer(group, tm):
        return (group, tm)

    nxt = peer(g, 2 * chip_at((pos + 1) % ring) + core)
    prv = peer(g, 2 * chip_at((pos + ring - 1) % ring) + core)
    mate = peer(g, 2 * chip + 1 - core)
    cross = peer(g + 1 - 2 * (g % 2), t)
    outside = t - 1 + 2 * core
    has_outside = (outside >= 0) & (outside < tiles)

    def remote(src, dst, ss, rs, dev):
        return pltpu.make_async_remote_copy(
            src_ref=src, dst_ref=dst, send_sem=ss, recv_sem=rs, device_id=dev, device_id_type=MESH
        )

    def normed(x, gain):
        x = x.astype(jnp.float32)
        inverse = lax.rsqrt(jnp.mean(x * x, axis=-1, keepdims=True) + 1e-06)
        return (x * inverse * gain).astype(jnp.bfloat16)

    step_rows = 32

    def normalise(src, src0, dst, dst0, gain):
        @pl.loop(0, rows // step_rows)
        def _(i):
            x = src[pl.ds(pl.multiple_of(src0 + i * step_rows, 16), step_rows), :]
            dst[pl.ds(pl.multiple_of(dst0 + i * step_rows, 16), step_rows), :] = normed(x, gain[...])

    normalise(q_ref, 0, qn, 0, qg_ref)
    normalise(k_ref, 0, kbuf, rows, kg_ref)

    barrier = pltpu.get_barrier_semaphore()
    for dev in (nxt, prv, mate, cross):
        pl.semaphore_signal(barrier, inc=1, device_id=dev, device_id_type=MESH)

    low, high = 4, 4 * (far - 1)
    base = jnp.where(t <= low, 6, high - 4)
    ends = (t == low) | (t == low - 1) | (t == high) | (t == high - 1)
    relays = (t // 2 == 3) | (t // 2 == (high - 4) // 2)
    served = jnp.where(t // 2 == 3, low - 1, high - 1)
    direct = has_outside & jnp.logical_not(ends)

    def greet(tm):
        pl.semaphore_signal(barrier, inc=1, device_id=peer(g, tm), device_id_type=MESH)

    pl.when(direct)(lambda: greet(outside))

    @pl.when(ends)
    def _():
        greet(base)
        greet(base + 1)

    @pl.when(relays)
    def _():
        greet(served)
        greet(served + 1)

    plain = jnp.logical_not(relays)
    pl.when(ends)(lambda: pl.semaphore_wait(barrier, 6))
    pl.when(relays)(lambda: pl.semaphore_wait(barrier, 7))
    pl.when(direct & plain)(lambda: pl.semaphore_wait(barrier, 5))
    pl.when(jnp.logical_not(has_outside))(lambda: pl.semaphore_wait(barrier, 4))

    def slot(number, start=0, size=rows):
        return pl.ds(pl.multiple_of(number * rows + start, 16), size)

    groups_of = 4 if heads % 4 == 0 else 1
    per = heads // groups_of

    def group_cols(i):
        return pl.ds(i * per * HD, per * HD)

    def pairs(i, number):
        cols = group_cols(i)
        return (
            (kbuf.at[slot(1), cols], kbuf.at[slot(number), cols]),
            (v_ref.at[:, cols], vbuf.at[slot(number), cols]),
        )

    def mate_halo(i, number):
        return [
            remote(src, dst, mate_ss.at[i, n], mate_rs.at[i, n], mate)
            for n, (src, dst) in enumerate(pairs(i, number))
        ]

    for i in range(groups_of):
        for c in mate_halo(i, 2 * core):
            c.start()

    def side_send(i):
        return [
            remote(src, dst, side_ss.at[i, n], side_rs.at[i, n], peer(g, outside))
            for n, (src, dst) in enumerate(pairs(i, 2 * (1 - core)))
        ]

    def side_recv(i):
        return [
            remote(dst, dst, side_ss.at[i, n], side_rs.at[i, n], cross)
            for n, (_, dst) in enumerate(pairs(i, 2 * core))
        ]

    def relay_in(i):
        return [
            remote(
                src, held.at[n, :, group_cols(i)], side_ss.at[i, n], relay_rs.at[i, n], peer(g, base + core)
            )
            for n, (src, _) in enumerate(pairs(i, 1))
        ]

    def relay_out(i):
        return [
            remote(
                held.at[n, :, group_cols(i)], dst, relay_ss.at[i, n], side_rs.at[i, n],
                peer(g, served + core),
            )
            for n, (_, dst) in enumerate(pairs(i, 2 * (1 - core)))
        ]

    def halo_issue(i):
        @pl.when(direct)
        def _():
            for c in side_send(i):
                c.start()

        @pl.when(ends)
        def _():
            for c in relay_in(i):
                c.start()

    def relay_step(i):
        @pl.when(relays)
        def _():
            for c, d in zip(relay_in(i), relay_out(i)):
                c.wait_recv()
                d.start()

    own_rows = pl.ds(pl.multiple_of(t * depth, 16), depth)
    own_cols = pl.ds(pl.multiple_of(col0, 128), half)
    local_w = pltpu.make_async_copy(w_ref.at[:, own_cols], wbuf.at[own_rows], local_sem.at[0])
    local_v = pltpu.make_async_copy(v_ref, vbuf.at[pl.ds(rows, rows)], local_sem.at[1])
    local_w.start()
    local_v.start()
    own_out = remote(w_ref.at[:, own_cols], wbuf.at[own_rows], own_ss, own_rs, mate)
    own_out.start()

    def shard_rows(d, s, c):
        place = (pos + (ring - s if d == 0 else s)) % ring
        return pl.ds(pl.multiple_of((2 * chip_at(place) + c) * depth, 16), depth)

    def used(d, s, q):
        return s < far or (s == far and q == d)

    def lanes(f, q):
        off, w = pieces[f]
        return pl.ds(off + q * w, w)

    def ring_send(d, f, s, q):
        off, w = pieces[f]
        if s == 1:
            src = w_ref.at[:, pl.ds(pl.multiple_of(col0 + off + q * w, 128), w)]
            where = own_rows
        else:
            where = shard_rows(d, s - 1, core)
            src = wbuf.at[where, lanes(f, q)]
        return remote(
            src, wbuf.at[where, lanes(f, q)], ring_ss.at[d, f, s - 1, q], ring_rs.at[d, f, s - 1, q],
            nxt if d == 0 else prv,
        )

    def ring_recv(d, f, s, q):
        here = wbuf.at[shard_rows(d, s, core), lanes(f, q)]
        return remote(here, here, ring_ss.at[d, f, s - 1, q], ring_rs.at[d, f, s - 1, q], nxt)

    def chip_copy(d, f, s, q, c):
        here = wbuf.at[shard_rows(d, s, c), lanes(f, q)]
        return remote(here, here, chip_ss.at[d, f, s - 1, q], chip_rs.at[d, f, s - 1, q], mate)

    def launch(f):
        for q in (0, 1):
            for d in (0, 1):
                if used(d, 1, q):
                    ring_send(d, f, 1, q).start()

    def ring_step(f, s):
        for q in (0, 1):
            for d in (0, 1):
                if used(d, s, q):
                    ring_recv(d, f, s, q).wait_recv()
                    if s < far and used(d, s + 1, q):
                        ring_send(d, f, s + 1, q).start()
                    chip_copy(d, f, s, q, core).start()
        if s == max(far - 1, 1) and f + 1 < len(pieces):
            launch(f + 1)


    see_before = (reach_ref[0, 0] == 1) & (t > 0)
    see_after = (reach_ref[0, 1] == 1) & (t < tiles - 1)
    column = lax.broadcasted_iota(jnp.int32, (1, 3 * rows), 1)
    lowest = jnp.where(see_before, 0, rows)
    highest = jnp.where(see_after, 3 * rows, 2 * rows)
    seen = (column >= lowest) & (column < highest)

    def head(h):
        at = pl.ds(pl.multiple_of(h * HD, 128), HD)
        logits = lax.dot_general(
            qn[:, at], kbuf[:, at], (((1,), (1,)), ((), ())), preferred_element_type=jnp.float32
        ) * (HD ** (-0.5))
        logits = jnp.where(seen, logits, -1e30)
        top = jnp.max(logits, axis=-1, keepdims=True)
        expo = jnp.exp(logits - top)
        weights = (expo * (1.0 / jnp.sum(expo, axis=-1, keepdims=True))).astype(jnp.bfloat16)
        att[0:rows, at] = jnp.dot(
            weights, vbuf[:, at], preferred_element_type=jnp.float32
        ).astype(jnp.bfloat16)

    def attention(i):
        @pl.loop(0, per)
        def _(j):
            head(i * per + j)

    def att_send(i):
        at = pl.ds(i * per * HD, per * HD)
        return remote(
            att.at[pl.ds(0, rows), at], att.at[pl.ds(rows, rows), at], att_ss.at[i], att_rs.at[i], cross
        )

    def wait_halo(i):
        for c in mate_halo(i, 2 * (1 - core)):
            c.wait_recv()

        @pl.when(has_outside)
        def _():
            for c in side_recv(i):
                c.wait_recv()

    def out_send(f):
        off, w = pieces[f]
        there = pl.ds(pl.multiple_of(col0 + off, 128), 2 * w)
        return remote(
            sbuf.at[:, pl.ds(off, 2 * w)], o_ref.at[:, there], out_ss.at[f], out_rs.at[f], cross
        )

    def out_recv(f):
        off, w = pieces[f]
        there = pl.ds(pl.multiple_of(half - col0 + off, 128), 2 * w)
        return remote(o_ref.at[:, there], o_ref.at[:, there], out_ss.at[f], out_rs.at[f], cross)

    def project(f):
        off, w = pieces[f]
        for s in range(1, far + 1):
            for q in (0, 1):
                for d in (0, 1):
                    if used(d, s, q):
                        chip_copy(d, f, s, q, 1 - core).wait_recv()
        block = 256

        @pl.loop(0, 2 * w // block)
        def _(j):
            at = pl.ds(pl.multiple_of(off + j * block, 128), block)
            out_at = pl.ds(pl.multiple_of(col0 + off + j * block, 128), block)
            total = jnp.dot(att[...], wbuf[:, at], preferred_element_type=jnp.float32)
            scaled = (gate_ref[:, out_at] * total).astype(jnp.bfloat16)
            sbuf[:, at] = scaled[rows:]
            o_ref[:, out_at] = scaled[:rows]

        out_send(f).start()

    queue = [(f, s) for f in range(len(pieces)) for s in range(1, far + 1)]
    started = taken = 0
    local_v.wait()

    @pl.when(jnp.logical_not(has_outside))
    def _():
        kbuf[slot(2 * core)] = jnp.zeros((rows, chans), jnp.bfloat16)
        vbuf[slot(2 * core)] = jnp.zeros((rows, chans), jnp.bfloat16)

    for act in SCHEDULE:
        if act == "L":
            launch(0)
        elif act == "R" and queue:
            ring_step(*queue.pop(0))
        elif act[0] == "H" and int(act[1]) < groups_of:
            halo_issue(int(act[1]))
        elif act[0] == "Y" and int(act[1]) < groups_of:
            relay_step(int(act[1]))
        elif act == "A" and taken < groups_of:
            wait_halo(taken)
            attention(taken)
            if taken > 0:
                att_send(taken - 1).start()
            taken += 1
        elif act == "S":
            att_send(groups_of - 1).start()
        elif act == "P" and started < len(pieces):
            while queue and queue[0][0] <= started:
                ring_step(*queue.pop(0))
            if started == 0:
                local_w.wait()
                remote(
                    w_ref.at[:, own_cols],
                    wbuf.at[pl.ds(pl.multiple_of((2 * chip + 1 - core) * depth, 16), depth)],
                    own_ss, own_rs, mate,
                ).wait_recv()
                for i in range(groups_of):
                    att_send(i).wait_recv()
            project(started)
            started += 1

    own_out.wait_send()
    for i in range(groups_of):
        for c in mate_halo(i, 2 * core):
            c.wait_send()

    @pl.when(has_outside)
    def _():
        for i in range(groups_of):
            for c in side_send(i):
                c.wait_send()

    @pl.when(relays)
    def _():
        for i in range(groups_of):
            for c in relay_out(i):
                c.wait_send()

    for i in range(groups_of):
        att_send(i).wait_send()
    for f in range(len(pieces)):
        for s in range(1, far + 1):
            for q in (0, 1):
                for d in (0, 1):
                    if used(d, s, q):
                        ring_send(d, f, s, q).wait_send()
                        chip_copy(d, f, s, q, core).wait_send()
    for f in range(len(pieces)):
        out_send(f).wait_send()
        out_recv(f).wait_recv()


def fused(peers, queries, keys, values, q_gain, k_gain, out_weight, out_gate, reach):
    rows, chans = queries.shape
    depth, wide = out_weight.shape
    half = wide // 2
    ring = peers // 2
    far = ring // 2
    parts = len(lane_pieces(half))
    groups_of = 4 if (chans // HD) % 4 == 0 else 1
    dma = pltpu.SemaphoreType.DMA
    vmem = pl.BlockSpec(memory_space=pltpu.VMEM)
    return pl.pallas_call(
        functools.partial(fused_kernel, ring),
        out_shape=jax.ShapeDtypeStruct((rows, wide), jnp.bfloat16),
        in_specs=[vmem] * 7 + [pl.BlockSpec(memory_space=pltpu.SMEM)],
        out_specs=vmem,
        scratch_shapes=[
            pltpu.VMEM((depth * peers, half), jnp.bfloat16),
            pltpu.VMEM((3 * rows, chans), jnp.bfloat16),
            pltpu.VMEM((3 * rows, chans), jnp.bfloat16),
            pltpu.VMEM((2, rows, chans), jnp.bfloat16),
            pltpu.VMEM((rows, chans), jnp.bfloat16),
            pltpu.VMEM((2 * rows, chans), jnp.bfloat16),
            pltpu.VMEM((rows, half), jnp.bfloat16),
            dma((2, parts, far, 2)),
            dma((2, parts, far, 2)),
            dma((2, parts, far, 2)),
            dma((2, parts, far, 2)),
            dma, dma,
            dma((groups_of, 2)), dma((groups_of, 2)), dma((groups_of, 2)), dma((groups_of, 2)),
            dma((groups_of, 2)), dma((groups_of, 2)),
            dma((groups_of,)), dma((groups_of,)),
            dma((parts,)), dma((parts,)),
            dma((2,)),
        ],
        compiler_params=pltpu.CompilerParams(
            collective_id=0, has_side_effects=True, vmem_limit_bytes=60 * 1024 * 1024
        ),
    )(
        queries, keys, values, q_gain.reshape(1, -1), k_gain.reshape(1, -1), out_weight,
        out_gate.reshape(1, -1), reach,
    )


def solution(mesh):
    groups, peers = mesh.shape["groups"], mesh.shape["tm"]

    def step(queries, keys, values, q_gain, k_gain, out_weight, out_gate, reach):
        fits = (
            groups % 2 == 0
            and peers % 4 == 0
            and peers >= 16
            and queries.shape[0] == TT * TH * TW
            and out_weight.shape[0] % 16 == 0
            and out_weight.shape[1] % 512 == 0
        )
        args = (queries, keys, values, q_gain, k_gain, out_weight, out_gate, reach)
        return fused(peers, *args) if fits else local(*args)

    return jax.shard_map(
        step,
        mesh=mesh,
        in_specs=(
            P(("groups", "tm"), None),
            P(("groups", "tm"), None),
            P(("groups", "tm"), None),
            P(),
            P(),
            P("tm", None),
            P(),
            P(("groups", "tm"), None),
        ),
        out_specs=P(("groups", "tm"), None),
        check_vma=False,
    )
```

```python
import functools

import jax
import jax.numpy as jnp
from jax import lax
from jax.experimental import pallas as pl
from jax.experimental.pallas import tpu as pltpu
from jax.sharding import PartitionSpec as P

HD = 128
TT = 4
TH = 6
TW = 8
MESH = pl.DeviceIdType.MESH
SCHEDULE = ("H0", "L", "H1", "H2", "H3", "R", "Y0", "R", "Y1", "A", "R", "Y2", "A", "R", "Y3", "A", "R", "A", "R", "S", "R", "P", "R", "R", "P", "R", "R", "P")


def shifted(shard, axis, by):
    peers = lax.axis_size(axis)
    pairs = [(i, i + by) for i in range(peers) if 0 <= i + by < peers]
    return lax.ppermute(shard, axis, pairs)


def rms_scaled(block, gain):
    values32 = block.astype(jnp.float32)
    inverse = lax.rsqrt(jnp.mean(values32 * values32, axis=-1, keepdims=True) + 1e-06)
    return (values32 * inverse * gain).astype(jnp.bfloat16)


def local(queries, keys, values, q_gain, k_gain, out_weight, out_gate, reach):
    tile = TT * TH * TW
    rows = queries.shape[0]
    chans = queries.shape[1]
    heads = chans // HD
    count = rows // tile
    scale = HD ** (-0.5)
    q_norm = rms_scaled(queries, q_gain)
    k_norm = rms_scaled(keys, k_gain)
    before_k, before_v = shifted((k_norm, values), "tm", 1)
    after_k, after_v = shifted((k_norm, values), "tm", -1)
    key_buffer = jnp.concatenate([before_k, k_norm, after_k], axis=0).reshape(
        count + 2, tile, heads, HD
    )
    val_buffer = jnp.concatenate([before_v, values, after_v], axis=0).reshape(
        count + 2, tile, heads, HD
    )
    position = lax.axis_index("tm")
    first_tile = position * count
    total_tiles = lax.axis_size("tm") * count
    global_tile = first_tile + jnp.arange(count, dtype=jnp.int32)
    valid = jnp.stack(
        [
            (reach[:, 0] == 1) & (global_tile > 0),
            global_tile >= 0,
            (reach[:, 1] == 1) & (global_tile < total_tiles - 1),
        ],
        axis=1,
    )
    query_tiles = q_norm.reshape(count, tile, heads, HD)
    seen_k = jnp.stack([key_buffer[offset : offset + count] for offset in range(3)], axis=1)
    seen_v = jnp.stack([val_buffer[offset : offset + count] for offset in range(3)], axis=1)
    logits = (
        jnp.einsum("nqhd,nokhd->nhqok", query_tiles, seen_k, preferred_element_type=jnp.float32)
        * scale
    )
    logits = jnp.where(valid[:, None, None, :, None], logits, -1e30)
    logits = logits.reshape(count, heads, tile, 3 * tile)
    top = jnp.max(logits, axis=-1, keepdims=True)
    expo = jnp.exp(logits - top)
    weights = (expo / jnp.sum(expo, axis=-1, keepdims=True)).astype(jnp.bfloat16)
    attended = jnp.einsum(
        "nhqk,nkhd->nqhd",
        weights,
        seen_v.reshape(count, 3 * tile, heads, HD),
        preferred_element_type=jnp.float32,
    ).astype(jnp.bfloat16)
    attended = attended.reshape(rows, chans)
    full_weight = lax.all_gather(out_weight, "tm", axis=0, tiled=True)
    projected = jnp.dot(attended, full_weight, preferred_element_type=jnp.float32)
    return (out_gate * projected).astype(jnp.bfloat16)


def lane_pieces(half):
    lanes = half // 256
    last = max(lanes // 5, 1)
    first = (lanes - last + 1) // 2
    widths = [w * 128 for w in (first, lanes - last - first, last) if w > 0]
    offsets, at = [], 0
    for w in widths:
        offsets.append(at)
        at += 2 * w
    return list(zip(offsets, widths))


def fused_kernel(
    ring, q_ref, k_ref, v_ref, qg_ref, kg_ref, w_ref, gate_ref, reach_ref, o_ref,
    wbuf, kbuf, vbuf, held, qn, att, sbuf,
    ring_ss, ring_rs, chip_ss, chip_rs, own_ss, own_rs, mate_ss, mate_rs, side_ss, side_rs, relay_ss, relay_rs,
    att_ss, att_rs, out_ss, out_rs, local_sem,
):
    rows, chans = q_ref.shape
    depth, wide = w_ref.shape
    half = wide // 2
    heads = chans // HD
    pieces = lane_pieces(half)
    far = ring // 2
    tiles = 2 * ring
    g, t = lax.axis_index("groups"), lax.axis_index("tm")
    core, chip = t % 2, t // 2
    row, col = chip // 2, chip % 2
    pos = row * (1 - col) + (ring - 1 - row) * col
    col0 = (g % 2) * half

    def chip_at(place):
        back = place // far
        line = place * (1 - back) + (ring - 1 - place) * back
        return 2 * line + back

    def peer(group, tm):
        return (group, tm)

    nxt = peer(g, 2 * chip_at((pos + 1) % ring) + core)
    prv = peer(g, 2 * chip_at((pos + ring - 1) % ring) + core)
    mate = peer(g, 2 * chip + 1 - core)
    cross = peer(g + 1 - 2 * (g % 2), t)
    outside = t - 1 + 2 * core
    has_outside = (outside >= 0) & (outside < tiles)

    def remote(src, dst, ss, rs, dev):
        return pltpu.make_async_remote_copy(
            src_ref=src, dst_ref=dst, send_sem=ss, recv_sem=rs, device_id=dev, device_id_type=MESH
        )

    def normed(x, gain):
        x = x.astype(jnp.float32)
        inverse = lax.rsqrt(jnp.mean(x * x, axis=-1, keepdims=True) + 1e-06)
        return (x * inverse * gain).astype(jnp.bfloat16)

    step_rows = 32

    def normalise(src, src0, dst, dst0, gain):
        @pl.loop(0, rows // step_rows)
        def _(i):
            x = src[pl.ds(pl.multiple_of(src0 + i * step_rows, 16), step_rows), :]
            dst[pl.ds(pl.multiple_of(dst0 + i * step_rows, 16), step_rows), :] = normed(x, gain[...].reshape(1, -1))

    normalise(q_ref, 0, qn, 0, qg_ref)
    normalise(k_ref, 0, kbuf, rows, kg_ref)

    barrier = pltpu.get_barrier_semaphore()
    for dev in (nxt, prv, mate, cross):
        pl.semaphore_signal(barrier, inc=1, device_id=dev, device_id_type=MESH)

    low, high = 4, 4 * (far - 1)
    base = jnp.where(t <= low, 6, high - 4)
    ends = (t == low) | (t == low - 1) | (t == high) | (t == high - 1)
    relays = (t // 2 == 3) | (t // 2 == (high - 4) // 2)
    served = jnp.where(t // 2 == 3, low - 1, high - 1)
    direct = has_outside & jnp.logical_not(ends)

    def greet(tm):
        pl.semaphore_signal(barrier, inc=1, device_id=peer(g, tm), device_id_type=MESH)

    pl.when(direct)(lambda: greet(outside))

    @pl.when(ends)
    def _():
        greet(base)
        greet(base + 1)

    @pl.when(relays)
    def _():
        greet(served)
        greet(served + 1)

    plain = jnp.logical_not(relays)
    pl.when(ends)(lambda: pl.semaphore_wait(barrier, 6))
    pl.when(relays)(lambda: pl.semaphore_wait(barrier, 7))
    pl.when(direct & plain)(lambda: pl.semaphore_wait(barrier, 5))
    pl.when(jnp.logical_not(has_outside))(lambda: pl.semaphore_wait(barrier, 4))

    def slot(number, start=0, size=rows):
        return pl.ds(pl.multiple_of(number * rows + start, 16), size)

    groups_of = 4 if heads % 4 == 0 else 1
    per = heads // groups_of

    def group_cols(i):
        return pl.ds(i * per * HD, per * HD)

    def pairs(i, number):
        cols = group_cols(i)
        return (
            (kbuf.at[slot(1), cols], kbuf.at[slot(number), cols]),
            (v_ref.at[:, cols], vbuf.at[slot(number), cols]),
        )

    def mate_halo(i, number):
        return [
            remote(src, dst, mate_ss.at[i, n], mate_rs.at[i, n], mate)
            for n, (src, dst) in enumerate(pairs(i, number))
        ]

    for i in range(groups_of):
        for c in mate_halo(i, 2 * core):
            c.start()

    def side_send(i):
        return [
            remote(src, dst, side_ss.at[i, n], side_rs.at[i, n], peer(g, outside))
            for n, (src, dst) in enumerate(pairs(i, 2 * (1 - core)))
        ]

    def side_recv(i):
        return [
            remote(dst, dst, side_ss.at[i, n], side_rs.at[i, n], cross)
            for n, (_, dst) in enumerate(pairs(i, 2 * core))
        ]

    def relay_in(i):
        return [
            remote(
                src, held.at[n, :, group_cols(i)], side_ss.at[i, n], relay_rs.at[i, n], peer(g, base + core)
            )
            for n, (src, _) in enumerate(pairs(i, 1))
        ]

    def relay_out(i):
        return [
            remote(
                held.at[n, :, group_cols(i)], dst, relay_ss.at[i, n], side_rs.at[i, n],
                peer(g, served + core),
            )
            for n, (_, dst) in enumerate(pairs(i, 2 * (1 - core)))
        ]

    def halo_issue(i):
        @pl.when(direct)
        def _():
            for c in side_send(i):
                c.start()

        @pl.when(ends)
        def _():
            for c in relay_in(i):
                c.start()

    def relay_step(i):
        @pl.when(relays)
        def _():
            for c, d in zip(relay_in(i), relay_out(i)):
                c.wait_recv()
                d.start()

    own_rows = pl.ds(pl.multiple_of(t * depth, 16), depth)
    own_cols = pl.ds(pl.multiple_of(col0, 128), half)
    local_w = pltpu.make_async_copy(w_ref.at[:, own_cols], wbuf.at[own_rows], local_sem.at[0])
    local_v = pltpu.make_async_copy(v_ref, vbuf.at[pl.ds(rows, rows)], local_sem.at[1])
    local_w.start()
    local_v.start()
    own_out = remote(w_ref.at[:, own_cols], wbuf.at[own_rows], own_ss, own_rs, mate)
    own_out.start()

    def shard_rows(d, s, c):
        place = (pos + (ring - s if d == 0 else s)) % ring
        return pl.ds(pl.multiple_of((2 * chip_at(place) + c) * depth, 16), depth)

    def used(d, s, q):
        return s < far or (s == far and q == d)

    def lanes(f, q):
        off, w = pieces[f]
        return pl.ds(off + q * w, w)

    def ring_send(d, f, s, q):
        off, w = pieces[f]
        if s == 1:
            src = w_ref.at[:, pl.ds(pl.multiple_of(col0 + off + q * w, 128), w)]
            where = own_rows
        else:
            where = shard_rows(d, s - 1, core)
            src = wbuf.at[where, lanes(f, q)]
        return remote(
            src, wbuf.at[where, lanes(f, q)], ring_ss.at[d, f, s - 1, q], ring_rs.at[d, f, s - 1, q],
            nxt if d == 0 else prv,
        )

    def ring_recv(d, f, s, q):
        here = wbuf.at[shard_rows(d, s, core), lanes(f, q)]
        return remote(here, here, ring_ss.at[d, f, s - 1, q], ring_rs.at[d, f, s - 1, q], nxt)

    def chip_copy(d, f, s, q, c):
        here = wbuf.at[shard_rows(d, s, c), lanes(f, q)]
        return remote(here, here, chip_ss.at[d, f, s - 1, q], chip_rs.at[d, f, s - 1, q], mate)

    def launch(f):
        for q in (0, 1):
            for d in (0, 1):
                if used(d, 1, q):
                    ring_send(d, f, 1, q).start()

    def ring_step(f, s):
        for q in (0, 1):
            for d in (0, 1):
                if used(d, s, q):
                    ring_recv(d, f, s, q).wait_recv()
                    if s < far and used(d, s + 1, q):
                        ring_send(d, f, s + 1, q).start()
                    chip_copy(d, f, s, q, core).start()
        if s == max(far - 1, 1) and f + 1 < len(pieces):
            launch(f + 1)


    see_before = (reach_ref[0, 0] == 1) & (t > 0)
    see_after = (reach_ref[0, 1] == 1) & (t < tiles - 1)
    column = lax.broadcasted_iota(jnp.int32, (1, 3 * rows), 1)
    lowest = jnp.where(see_before, 0, rows)
    highest = jnp.where(see_after, 3 * rows, 2 * rows)
    seen = (column >= lowest) & (column < highest)

    def head(h):
        at = pl.ds(pl.multiple_of(h * HD, 128), HD)
        logits = lax.dot_general(
            qn[:, at], kbuf[:, at], (((1,), (1,)), ((), ())), preferred_element_type=jnp.float32
        ) * (HD ** (-0.5))
        logits = jnp.where(seen, logits, -1e30)
        top = jnp.max(logits, axis=-1, keepdims=True)
        expo = jnp.exp(logits - top)
        weights = (expo * (1.0 / jnp.sum(expo, axis=-1, keepdims=True))).astype(jnp.bfloat16)
        att[0:rows, at] = jnp.dot(
            weights, vbuf[:, at], preferred_element_type=jnp.float32
        ).astype(jnp.bfloat16)

    def attention(i):
        @pl.loop(0, per)
        def _(j):
            head(i * per + j)

    def att_send(i):
        at = pl.ds(i * per * HD, per * HD)
        return remote(
            att.at[pl.ds(0, rows), at], att.at[pl.ds(rows, rows), at], att_ss.at[i], att_rs.at[i], cross
        )

    def wait_halo(i):
        for c in mate_halo(i, 2 * (1 - core)):
            c.wait_recv()

        @pl.when(has_outside)
        def _():
            for c in side_recv(i):
                c.wait_recv()

    def out_send(f):
        off, w = pieces[f]
        there = pl.ds(pl.multiple_of(col0 + off, 128), 2 * w)
        return remote(
            sbuf.at[:, pl.ds(off, 2 * w)], o_ref.at[:, there], out_ss.at[f], out_rs.at[f], cross
        )

    def out_recv(f):
        off, w = pieces[f]
        there = pl.ds(pl.multiple_of(half - col0 + off, 128), 2 * w)
        return remote(o_ref.at[:, there], o_ref.at[:, there], out_ss.at[f], out_rs.at[f], cross)

    def project(f):
        off, w = pieces[f]
        for s in range(1, far + 1):
            for q in (0, 1):
                for d in (0, 1):
                    if used(d, s, q):
                        chip_copy(d, f, s, q, 1 - core).wait_recv()
        block = 256

        @pl.loop(0, 2 * w // block)
        def _(j):
            at = pl.ds(pl.multiple_of(off + j * block, 128), block)
            out_at = pl.ds(pl.multiple_of(col0 + off + j * block, 128), block)
            total = jnp.dot(att[...], wbuf[:, at], preferred_element_type=jnp.float32)
            scaled = (gate_ref[:, out_at] * total).astype(jnp.bfloat16)
            sbuf[:, at] = scaled[rows:]
            o_ref[:, out_at] = scaled[:rows]

        out_send(f).start()

    queue = [(f, s) for f in range(len(pieces)) for s in range(1, far + 1)]
    started = taken = 0
    local_v.wait()

    @pl.when(jnp.logical_not(has_outside))
    def _():
        kbuf[slot(2 * core)] = jnp.zeros((rows, chans), jnp.bfloat16)
        vbuf[slot(2 * core)] = jnp.zeros((rows, chans), jnp.bfloat16)

    for act in SCHEDULE:
        if act == "L":
            launch(0)
        elif act == "R" and queue:
            ring_step(*queue.pop(0))
        elif act[0] == "H" and int(act[1]) < groups_of:
            halo_issue(int(act[1]))
        elif act[0] == "Y" and int(act[1]) < groups_of:
            relay_step(int(act[1]))
        elif act == "A" and taken < groups_of:
            wait_halo(taken)
            attention(taken)
            if taken > 0:
                att_send(taken - 1).start()
            taken += 1
        elif act == "S":
            att_send(groups_of - 1).start()
        elif act == "P" and started < len(pieces):
            while queue and queue[0][0] <= started:
                ring_step(*queue.pop(0))
            if started == 0:
                local_w.wait()
                remote(
                    w_ref.at[:, own_cols],
                    wbuf.at[pl.ds(pl.multiple_of((2 * chip + 1 - core) * depth, 16), depth)],
                    own_ss, own_rs, mate,
                ).wait_recv()
                for i in range(groups_of):
                    att_send(i).wait_recv()
            project(started)
            started += 1

    own_out.wait_send()
    for i in range(groups_of):
        for c in mate_halo(i, 2 * core):
            c.wait_send()

    @pl.when(has_outside)
    def _():
        for i in range(groups_of):
            for c in side_send(i):
                c.wait_send()

    @pl.when(relays)
    def _():
        for i in range(groups_of):
            for c in relay_out(i):
                c.wait_send()

    for i in range(groups_of):
        att_send(i).wait_send()
    for f in range(len(pieces)):
        for s in range(1, far + 1):
            for q in (0, 1):
                for d in (0, 1):
                    if used(d, s, q):
                        ring_send(d, f, s, q).wait_send()
                        chip_copy(d, f, s, q, core).wait_send()
    for f in range(len(pieces)):
        out_send(f).wait_send()
        out_recv(f).wait_recv()


def fused(peers, queries, keys, values, q_gain, k_gain, out_weight, out_gate, reach):
    rows, chans = queries.shape
    depth, wide = out_weight.shape
    half = wide // 2
    ring = peers // 2
    far = ring // 2
    parts = len(lane_pieces(half))
    groups_of = 4 if (chans // HD) % 4 == 0 else 1
    dma = pltpu.SemaphoreType.DMA
    vmem = pl.BlockSpec(memory_space=pltpu.VMEM)
    return pl.pallas_call(
        functools.partial(fused_kernel, ring),
        out_shape=jax.ShapeDtypeStruct((rows, wide), jnp.bfloat16),
        in_specs=[vmem] * 7 + [pl.BlockSpec(memory_space=pltpu.SMEM)],
        out_specs=vmem,
        scratch_shapes=[
            pltpu.VMEM((depth * peers, half), jnp.bfloat16),
            pltpu.VMEM((3 * rows, chans), jnp.bfloat16),
            pltpu.VMEM((3 * rows, chans), jnp.bfloat16),
            pltpu.VMEM((2, rows, chans), jnp.bfloat16),
            pltpu.VMEM((rows, chans), jnp.bfloat16),
            pltpu.VMEM((2 * rows, chans), jnp.bfloat16),
            pltpu.VMEM((rows, half), jnp.bfloat16),
            dma((2, parts, far, 2)),
            dma((2, parts, far, 2)),
            dma((2, parts, far, 2)),
            dma((2, parts, far, 2)),
            dma, dma,
            dma((groups_of, 2)), dma((groups_of, 2)), dma((groups_of, 2)), dma((groups_of, 2)),
            dma((groups_of, 2)), dma((groups_of, 2)),
            dma((groups_of,)), dma((groups_of,)),
            dma((parts,)), dma((parts,)),
            dma((2,)),
        ],
        compiler_params=pltpu.CompilerParams(
            collective_id=0, has_side_effects=True, vmem_limit_bytes=60 * 1024 * 1024
        ),
    )(
        queries, keys, values, q_gain, k_gain, out_weight,
        out_gate.reshape(1, -1), reach,
    )


def solution(mesh):
    groups, peers = mesh.shape["groups"], mesh.shape["tm"]

    def step(queries, keys, values, q_gain, k_gain, out_weight, out_gate, reach):
        fits = (
            groups % 2 == 0
            and peers % 4 == 0
            and peers >= 16
            and queries.shape[0] == TT * TH * TW
            and out_weight.shape[0] % 16 == 0
            and out_weight.shape[1] % 512 == 0
        )
        args = (queries, keys, values, q_gain, k_gain, out_weight, out_gate, reach)
        return fused(peers, *args) if fits else local(*args)

    return jax.shard_map(
        step,
        mesh=mesh,
        in_specs=(
            P(("groups", "tm"), None),
            P(("groups", "tm"), None),
            P(("groups", "tm"), None),
            P(),
            P(),
            P("tm", None),
            P(),
            P(("groups", "tm"), None),
        ),
        out_specs=P(("groups", "tm"), None),
        check_vma=False,
    )
```
